32 devices in a mesh: groups: 2 (over x), seq: 16 (over z, y, core).
Axes of the slice: x: 2, y: 2, z: 4, core: 2. Of those that a mesh axis runs over, the one named last changes fastest.
Arguments:
- features: bfloat16 [8192, 1536], P(('groups', 'seq')), parts along dimension 0, may hold values from -6 to 6
- cotangent: bfloat16 [8192, 1536], P(('groups', 'seq')), parts along dimension 0, may hold values from -6 to 6
- dilated_kernel_weight: bfloat16 [2, 3, 1536, 768], replicated, may hold values from -0.09375 to 0.09375
- out_weight: bfloat16 [2, 768, 1536], replicated, may hold values from -0.21875 to 0.21875
- scale_inner: float32 [2, 1536], replicated, may hold values from 0.5 to 2
- inner_norm_offset: float32 [2, 1536], replicated, may hold values from -3 to 3
- scale_middle: float32 [2, 768], replicated, may hold values from 0.5 to 2
- shift_middle: float32 [2, 768], replicated, may hold values from -3 to 3
Outputs:
- block_out: bfloat16 [8192, 1536], P(('groups', 'seq')), parts along dimension 0
- feature_grad: bfloat16 [8192, 1536], P(('groups', 'seq')), parts along dimension 0
- conv_grad: float32 [4, 3, 1536, 768], P('groups', None, 'seq'), parts along dimension 0
- out_grad: float32 [4, 768, 1536], P('groups', None, 'seq'), parts along dimension 0
The draws below stay inside these ranges and needn't reach their ends.
There are 2 independent parts, one for each index of `groups`. The reference program is written for one: setup_inputs(seed, part) draws one part's arguments, and reference() takes and returns one part's arrays. A program takes and returns all parts, laid end to end along the dimension named above; an argument that names none is the same for every part. Nothing has to cross between parts.
All inputs are finite; a program needn't handle non-finite values.
Results may differ from the reference program's by a relative error of at most 0.02.
Values may be sent and summed in bfloat16 or wider, within the bound.
A program may use at most 128 MiB of HBM per device.

```python
import math
import jax
import jax.numpy as jnp
from jax import lax

C = 1536
H = 768
FIRST_SPACING = 512
SECOND_SPACING = 2048
BINS = 4096
N_SEQ = 16


def raised(array, key, source, target, parts, factor):
    owner, partner = [(jnp.arange(array.shape[dim]) // (array.shape[dim] // parts)).reshape([-1 if axis == dim else 1 for axis in range(array.ndim)]) for dim in (source, target)]
    chosen = jax.random.permutation(key, parts)[partner]
    strong = (owner == chosen) | (owner == (partner + parts // 2) % parts)
    return jnp.where(strong, factor * array, array)


def level_of(key, shape, split, smallest, top_value):
    gain = 1.0
    for dim, parts in split:
        steps = jax.random.uniform(jax.random.fold_in(jax.random.fold_in(key, 6), dim), (parts,), jnp.float32, smallest / len(split), top_value / len(split))
        gain = gain * jnp.repeat(jnp.exp(steps), shape[dim] // parts).reshape((-1,) + (1,) * (len(shape) - 1 - dim))
    return gain


def normal_values(rng, dims, deviation, most, pieces=(), held_as=jnp.bfloat16):
    drawn = deviation * jax.random.normal(rng, dims, jnp.float32)
    if pieces:
        drawn = drawn * level_of(rng, dims, pieces, -0.22, 0.18)
    return jnp.clip(drawn, -most, most).astype(held_as)


def noise_with(own_key, dims, width, most, pieces, heavy, dtype=jnp.bfloat16):
    drawn = width * jax.random.normal(own_key, dims, jnp.float32)
    if pieces:
        drawn = drawn * level_of(own_key, dims, pieces, -0.22, 0.18)
    return jnp.clip(raised(drawn, jax.random.fold_in(own_key, 3), *heavy), -most, most).astype(dtype)


def setup_inputs(seed: int = 0, part: int = 0) -> dict:
    keys = jax.random.split(jax.random.key(seed), 9)
    part_splits = jax.random.split(jax.random.fold_in(keys[8], part), 9)
    return {
        "features": noise_with(part_splits[0], (BINS, C), 1.0, 6.0, ((0, 16),), (0, 1, 16, 2.0)),
        "cotangent": noise_with(part_splits[1], (BINS, C), 1.0, 6.0, ((0, 16),), (0, 1, 16, 2.0)),
        "dilated_kernel_weight": normal_values(keys[2], (2, 3, C, H), (3 * C) ** -0.5, 0.09375),
        "out_weight": normal_values(keys[3], (2, H, C), H ** -0.5, 0.21875),
        "scale_inner": jnp.clip(jnp.exp(jax.random.uniform(keys[4], (2, C), jnp.float32, math.log(0.5), math.log(2.0))), 0.5, 2.0),
        "inner_norm_offset": normal_values(keys[5], (2, C), 0.5, 3.0, (), jnp.float32),
        "scale_middle": jnp.clip(jnp.exp(jax.random.uniform(keys[6], (2, H), jnp.float32, math.log(0.5), math.log(2.0))), 0.5, 2.0),
        "shift_middle": normal_values(keys[7], (2, H), 0.5, 3.0, (), jnp.float32),
    }


def gelu_tanh(inputs):
    return jax.nn.gelu(inputs, approximate=True)

def gelu_back(inputs, upstream):
    primal, pullback = jax.vjp(gelu_tanh, inputs)
    return pullback(upstream)[0]

def shifted(values, offset):
    length = values.shape[0]
    if abs(offset) >= length:
        return jnp.zeros_like(values)
    if offset > 0:
        return jnp.concatenate([values[offset:], jnp.zeros_like(values[:offset])], axis=0)
    if offset < 0:
        return jnp.concatenate([jnp.zeros_like(values[offset:]), values[:offset]], axis=0)
    return values

def blockwise(left_rows, right_rows):
    per_shard_portion = left_rows.shape[0] // N_SEQ
    left_blocks = left_rows.astype(jnp.float32).reshape(N_SEQ, per_shard_portion, left_rows.shape[1])
    right_blocks = right_rows.astype(jnp.float32).reshape(N_SEQ, per_shard_portion, right_rows.shape[1])
    partial_value = jnp.einsum('bjc,bjh->bch', left_blocks, right_blocks)
    rounded = lax.optimization_barrier(partial_value.astype(jnp.bfloat16))
    return lax.optimization_barrier(jnp.sum(rounded.astype(jnp.float32), axis=0))

def reference(features, cotangent, dilated_kernel_weight, out_weight, scale_inner, inner_norm_offset, scale_middle, shift_middle):
    spacing_per_layer = (FIRST_SPACING, SECOND_SPACING)
    current = features
    stored = []
    for layer_index in range(2):
        dilation = spacing_per_layer[layer_index]
        inner_pre = scale_inner[layer_index] * current.astype(jnp.float32) + inner_norm_offset[layer_index]
        activated = gelu_tanh(inner_pre).astype(jnp.bfloat16)
        conv_sum = jnp.zeros((activated.shape[0], H), jnp.float32)
        for tap_index in range(3):
            conv_sum = conv_sum + jnp.dot(shifted(activated, (tap_index - 1) * dilation), dilated_kernel_weight[layer_index, tap_index], preferred_element_type=jnp.float32)
        middle_pre = scale_middle[layer_index] * conv_sum + shift_middle[layer_index]
        middle = gelu_tanh(middle_pre).astype(jnp.bfloat16)
        stored.append((inner_pre, activated, middle_pre, middle))
        current = (current.astype(jnp.float32) + jnp.dot(middle, out_weight[layer_index], preferred_element_type=jnp.float32)).astype(jnp.bfloat16)
    grad_out = cotangent
    conv_grads = [None, None]
    out_grads = [None, None]
    for layer_index in (1, 0):
        dilation = spacing_per_layer[layer_index]
        inner_pre, activated, middle_pre, middle = stored[layer_index]
        grad_middle = jnp.dot(grad_out, out_weight[layer_index].T, preferred_element_type=jnp.float32)
        out_grads[layer_index] = blockwise(middle, grad_out)
        grad_conv = (gelu_back(middle_pre, grad_middle) * scale_middle[layer_index]).astype(jnp.bfloat16)
        activated_gradient = jnp.zeros((grad_conv.shape[0], C), jnp.float32)
        tap_terms = []
        for tap_index in range(3):
            shifted_grad = shifted(grad_conv, -(tap_index - 1) * dilation)
            activated_gradient = activated_gradient + jnp.dot(shifted_grad, dilated_kernel_weight[layer_index, tap_index].T, preferred_element_type=jnp.float32)
            tap_terms.append(blockwise(activated, shifted_grad))
        conv_grads[layer_index] = jnp.stack(tap_terms)
        grad_out = (grad_out.astype(jnp.float32) + gelu_back(inner_pre, activated_gradient) * scale_inner[layer_index]).astype(jnp.bfloat16)
    return (current, grad_out, jnp.stack(conv_grads), jnp.stack(out_grads))
```

```python
import jax
import jax.numpy as jnp
from jax import lax
from jax.sharding import PartitionSpec as P

SPACINGS = (512, 2048)
QUAD = 4
F32 = jnp.float32
BF16 = jnp.bfloat16


def gelu_tanh(inputs):
    return jax.nn.gelu(inputs, approximate=True)


def gelu_back(inputs, upstream):
    primal, pullback = jax.vjp(gelu_tanh, inputs)
    return pullback(upstream)[0]


def dot(a, b):
    return jnp.dot(a, b, preferred_element_type=F32)


def dot_t(a, b):
    return jnp.einsum("jh,ch->jc", a, b, preferred_element_type=F32)


def on_device(
    features,
    cotangent,
    dilated_kernel_weight,
    out_weight,
    scale_inner,
    inner_norm_offset,
    scale_middle,
    shift_middle,
):
    rows, channels = features.shape
    hidden = out_weight.shape[1]
    n = lax.axis_size("seq")
    lanes = SPACINGS[0] // rows
    members = n // lanes
    chunk = rows // members
    mix_groups = [[i for i in range(n) if i % lanes == r] for r in range(lanes)]
    tall = n // QUAD
    own = channels // n

    def remix(x):
        return lax.all_to_all(x, "seq", 0, 0, axis_index_groups=mix_groups, tiled=True)

    me = lax.axis_index("seq")
    core = me % 2
    side = me // 2 % 2
    up = me // QUAD

    def swap(x, bit):
        return lax.ppermute(x, "seq", [(i, i ^ bit) for i in range(n)])

    def quad_gather(x):
        pair = jnp.stack([x, swap(x, 2)])
        return jnp.concatenate([pair, swap(pair, 1)])

    def quad_parts(x):
        parts = x.T.reshape(tall, 2, 2, own, rows).transpose(1, 2, 0, 3, 4)
        parts = parts.reshape(2, 2, tall * own, rows)
        take = lambda v, i: lax.dynamic_index_in_dim(v, i, 0, keepdims=False)
        pair = jnp.stack([take(parts, side), swap(take(parts, 1 - side), 2)], axis=1)
        return jnp.concatenate([take(pair, core), swap(take(pair, 1 - core), 1)])

    def reduce(x):
        x = x.reshape(-1, tall, own, hidden)
        bit = 1
        take = lambda v, i: lax.dynamic_index_in_dim(v, i, 2, keepdims=False)
        while bit < tall:
            x = x.reshape(x.shape[0], -1, 2, *([own, hidden]))
            keep = up // bit % 2
            sent = swap(take(x, 1 - keep).astype(BF16), QUAD * bit)
            x = take(x, keep) + sent.astype(F32)
            bit *= 2
        return x[:, 0]

    def lower(y, s):
        return jnp.pad(y, ((s, 0), (0, 0)))

    def raiser(y, s):
        return jnp.pad(y, ((0, s), (0, 0)))

    def outer(a, b):
        return jnp.einsum("qcj,qjh->ch", a, b, preferred_element_type=F32)

    def finish(pending, layer, conv_grads, out_grads):
        first = reduce(jnp.stack(pending[0]))
        rest = reduce(jnp.stack(pending[1]))
        out_grads[layer] = first[0].T
        conv_grads[layer] = jnp.stack([rest[0], first[1], rest[1]])

    tie = lax.optimization_barrier

    current, cotangent = tie((remix(features), cotangent))
    grad_out = remix(cotangent)
    stored = []
    for layer in range(2):
        s = SPACINGS[layer] // SPACINGS[0] * chunk
        w = dilated_kernel_weight[layer]
        inner_pre = scale_inner[layer] * current.astype(F32) + inner_norm_offset[layer]
        activated = gelu_tanh(inner_pre).astype(BF16)
        conv_sum = (
            dot(activated, w[1])
            + lower(dot(activated[:-s], w[0]), s)
            + raiser(dot(activated[s:], w[2]), s)
        )
        middle_pre = scale_middle[layer] * conv_sum + shift_middle[layer]
        middle = gelu_tanh(middle_pre).astype(BF16)
        stored.append([current, quad_parts(activated), middle_pre, quad_gather(middle)])
        current = (current.astype(F32) + dot(middle, out_weight[layer])).astype(BF16)
    grad_out, current, stored[0][1], stored[0][3] = tie(
        (grad_out, current, stored[0][1], stored[0][3])
    )
    block_out = remix(current)
    conv_grads = [None, None]
    out_grads = [None, None]
    pending = None
    for layer in (1, 0):
        s = SPACINGS[layer] // SPACINGS[0] * chunk
        w = dilated_kernel_weight[layer]
        entered, act_q, middle_pre, middle_q = stored[layer]
        inner_pre = scale_inner[layer] * entered.astype(F32) + inner_norm_offset[layer]
        grad_middle = dot_t(grad_out, out_weight[layer])
        grad_conv = (gelu_back(middle_pre, grad_middle) * scale_middle[layer]).astype(BF16)
        go_q = quad_parts(grad_out)
        g_q = quad_gather(grad_conv)
        if pending is not None:
            grad_conv, pending = tie((grad_conv, pending))
            block_out, grad_conv = tie((block_out, grad_conv))
            finish(pending, 1, conv_grads, out_grads)
        grad_active = (
            dot_t(grad_conv, w[1])
            + raiser(dot_t(grad_conv[s:], w[0]), s)
            + lower(dot_t(grad_conv[:-s], w[2]), s)
        )
        grad_out = (
            grad_out.astype(F32) + gelu_back(inner_pre, grad_active) * scale_inner[layer]
        ).astype(BF16)
        pending = (
            (outer(go_q, middle_q), outer(act_q, g_q)),
            (outer(act_q[:, :, :-s], g_q[:, s:]), outer(act_q[:, :, s:], g_q[:, :-s])),
        )
    feature_grad = remix(grad_out)
    finish(pending, 0, conv_grads, out_grads)
    return (block_out, feature_grad, jnp.stack(conv_grads), jnp.stack(out_grads))


def solution(mesh):
    rows = P(("groups", "seq"), None)
    return jax.shard_map(
        on_device,
        mesh=mesh,
        in_specs=(rows, rows, P(), P(), P(), P(), P(), P()),
        out_specs=(rows, rows, P("groups", None, "seq", None), P("groups", None, "seq")),
        check_vma=False,
    )
```
